32 devices in a mesh: prow: 8 (over z, core), pcol: 4 (over y, x).
Axes of the slice: x: 2, y: 2, z: 4, core: 2. Of those that a mesh axis runs over, the one named last changes fastest.
Arguments:
- diag_block: float32 [256, 256], P('prow', 'pcol'), as said below
- panel: float32 [16384, 256], P('prow', 'pcol'), may hold values from -1.5 to 1.5
- slab: float32 [16384, 1024], P('prow', 'pcol'), may hold values from -6 to 6
Outputs:
- diag_factor: float32 [256, 256], P('prow', 'pcol')
- panel_factor: float32 [16384, 256], P('prow', 'pcol')
- slab_updated: float32 [16384, 1024], P('prow', 'pcol')
The draws below stay inside these ranges and needn't reach their ends.
Inputs may be any that keep to these rules, and one draw needn't show every extreme that they name: diag_block is symmetric positive definite.
All inputs are finite; a program needn't handle non-finite values.
Results may differ from the reference program's by a relative error of at most 0.0003.
Values sent between devices are 32-bit elements; how exact they have to be, the bound alone decides.
A program may use at most 64 MiB of HBM per device.

```python
import jax
import jax.numpy as jnp
from jax import lax

B = 256
LB = 8
PANEL = 16384
SLAB = 1024
N_PROW = 8
N_PCOL = 4


def draw_diag_block(key, part):
    base = jax.random.normal(jax.random.fold_in(key, 11), (B, B), jnp.float32)
    matrix = 2.0 * jnp.eye(B, dtype=jnp.float32) + jnp.dot(base, base.T) / B
    return 0.5 * (matrix + matrix.T)


def block_scale(rng, dims, shards, least, largest):
    loudness = 1.0
    for position, blocks in shards:
        draws = jax.random.uniform(jax.random.fold_in(jax.random.fold_in(rng, 6), position), (blocks,), jnp.float32, least / len(shards), largest / len(shards))
        loudness = loudness * jnp.repeat(jnp.exp(draws), dims[position] // blocks).reshape((-1,) + (1,) * (len(dims) - 1 - position))
    return loudness


def scatter_about(key, shape, deviation, bound, pieces=(), held_as=jnp.bfloat16):
    loudness = block_scale(key, shape, pieces, -0.22, 0.18) if pieces else 1.0
    array = jax.random.normal(key, shape, jnp.float32) * deviation * loudness
    return jnp.minimum(jnp.maximum(array, -bound), bound).astype(held_as)


def setup_inputs(seed: int = 0) -> dict:
    splits = jax.random.split(jax.random.key(seed), 4)
    diag_block = draw_diag_block(jax.random.fold_in(splits[3], 71), 0)
    panel = scatter_about(splits[1], (PANEL, B), 0.25, 1.5, ((0, 8), (1, 4)), jnp.float32)
    slab = scatter_about(splits[2], (PANEL, SLAB), 1.0, 6.0, ((0, 8), (1, 4)), jnp.float32)
    return {"diag_block": diag_block, "panel": panel, "slab": slab}


def reference(diag_block, panel, slab):
    diag_factor = jnp.linalg.cholesky(diag_block)
    panel_factor = jax.scipy.linalg.solve_triangular(diag_factor, panel.T, lower=True).T
    blocks = panel_factor.reshape(N_PROW * LB, B, B)
    group = LB * N_PROW // N_PCOL
    targets = jnp.arange(N_PCOL, dtype=jnp.int32) * group
    array_blocks = targets % N_PROW * LB + targets // N_PROW
    column_blocks = blocks[array_blocks]
    index = jnp.arange(PANEL, dtype=jnp.int32)
    block_index = index // B
    row_global = (block_index % LB * N_PROW + block_index // LB) * B + index % B
    slab_blocks = jnp.transpose(slab.reshape(PANEL, N_PCOL, B), (1, 0, 2))
    inner = jnp.arange(B, dtype=jnp.int32)

    def update(items):
        column_rows, slab_here, target = items
        product = jnp.dot(panel_factor.astype(jnp.float32), column_rows.T.astype(jnp.float32), precision=lax.Precision.HIGHEST, preferred_element_type=jnp.float32)
        col_global = target * B + inner
        keep_mask = row_global[:, None] >= col_global[None, :]
        return jnp.where(keep_mask, slab_here - product, slab_here)
    updated = lax.map(update, (column_blocks, slab_blocks, targets))
    slab_updated = jnp.transpose(updated, (1, 0, 2)).reshape(PANEL, SLAB)
    return (diag_factor, panel_factor, slab_updated)
```

```python
import functools

import jax
import jax.numpy as jnp
from jax import lax
from jax.experimental import pallas as pl
from jax.experimental.pallas import tpu as pltpu
from jax.sharding import PartitionSpec as P

HI = lax.Precision.HIGHEST
F32 = jnp.float32
NB = 64


def small(groups, width):
    sub = lax.broadcasted_iota(jnp.int32, (8, 1), 0)
    for j in range(width):
        first, inner = divmod(j, 8)
        row = groups[first][inner : inner + 1, :]
        scale = lax.rsqrt(row[:, j : j + 1])
        row = row * scale
        for g in range(first, width // 8):
            column = groups[g][:, j : j + 1] * scale
            if g == first:
                column = jnp.where(sub > inner, column, 0.0)
                groups[g] = jnp.where(sub == inner, row, groups[g] - column * row)
            else:
                groups[g] = groups[g] - column * row
    return groups


def factor_block(work, upper, size, width, b):
    start, end = b * width, (b + 1) * width
    eye = (
        lax.broadcasted_iota(jnp.int32, (width, width), 0)
        == lax.broadcasted_iota(jnp.int32, (width, width), 1)
    ).astype(F32)
    both = jnp.concatenate([work[start:end, start:end], eye], axis=1)
    groups = small([both[8 * g : 8 * g + 8] for g in range(width // 8)], width)
    inverse = jnp.concatenate(groups, axis=0)[:, width:]
    rows = jnp.dot(inverse, work[start:end, :], precision=HI, preferred_element_type=F32)
    keep = (
        lax.broadcasted_iota(jnp.int32, (width, size), 1)
        >= lax.broadcasted_iota(jnp.int32, (width, size), 0) + start
    )
    left = jnp.where(keep, rows[:, :size], 0.0)
    upper[start:end, :] = left
    work[start:end, size:] = rows[:, size:]
    if end < size:
        column = left.T[end:, :]
        work[end:, :] = work[end:, :] - jnp.dot(
            column,
            jnp.concatenate([left, rows[:, size:]], axis=1),
            precision=HI,
            preferred_element_type=F32,
        )


def gather_kernel(
    rows, cols, group,
    diag, panel,
    gathered, lower, inverse, strip,
    tiles, work, upper, strip_in, strip_all,
    tile_send, tile_recv, wide_send, wide_recv, own_sem,
    panel_send, panel_recv, strip_send, strip_recv, ex_send, ex_recv, copy_sem,
):
    row, col = lax.axis_index("prow"), lax.axis_index("pcol")
    size = upper.shape[0]

    def down(d):
        return {"prow": lax.rem(row + d, rows)}

    def across(d):
        return {"pcol": lax.rem(col + d, cols)}

    def remote(src, dst, send, recv, to):
        return pltpu.make_async_remote_copy(
            src_ref=src, dst_ref=dst, send_sem=send, recv_sem=recv,
            device_id=to, device_id_type=pl.DeviceIdType.MESH,
        )

    barrier = pltpu.get_barrier_semaphore()
    for d in range(1, rows):
        pl.semaphore_signal(barrier, inc=1, device_id=down(d), device_id_type=pl.DeviceIdType.MESH)
    for d in range(1, cols):
        pl.semaphore_signal(barrier, inc=1, device_id=across(d), device_id_type=pl.DeviceIdType.MESH)
    own_tile = pltpu.make_async_copy(diag, tiles.at[col, row], own_sem.at[0])
    own_tile.start()
    own_panel = pltpu.make_async_copy(panel, gathered.at[col], own_sem.at[1])
    own_panel.start()
    pl.semaphore_wait(barrier, rows + cols - 2)

    tile_copies = [
        remote(diag, tiles.at[col, row], tile_send.at[d], tile_recv.at[d], down(d))
        for d in range(1, rows)
    ]
    for copy in tile_copies:
        copy.start()
    own_tile.wait()
    for copy in tile_copies:
        copy.wait()
    wide = [
        remote(tiles.at[col], tiles.at[col], wide_send.at[d], wide_recv.at[d], across(d))
        for d in range(1, cols)
    ]
    for copy in wide:
        copy.start()

    def strip_block(c):
        return panel.at[pl.ds((c * group // rows) * size, size)]

    def strip_copy(c, d):
        return remote(
            strip_block(c), strip_in.at[c], strip_send.at[c, d], strip_recv.at[c], down(d)
        )

    for c in range(cols):
        root = (c * group) % rows

        @pl.when(row == root)
        def _():
            pltpu.make_async_copy(strip_block(c), strip_in.at[c], copy_sem.at[c]).start()
            for d in range(1, rows):
                strip_copy(c, d).start()

    for copy in wide:
        copy.wait()
    panels = [
        remote(panel, gathered.at[col], panel_send.at[d], panel_recv.at[d], across(d))
        for d in range(1, cols)
    ]
    for copy in panels:
        copy.start()

    for c in range(cols):
        for r in range(rows):
            high, low = tiles.shape[2], tiles.shape[3]
            work[r * high : (r + 1) * high, c * low : (c + 1) * low] = tiles[c, r]
    work[:, size:] = (
        lax.broadcasted_iota(jnp.int32, (size, size), 0)
        == lax.broadcasted_iota(jnp.int32, (size, size), 1)
    ).astype(F32)

    blocks = size // NB
    exchange = [
        remote(
            strip_in.at[lax.rem(col + d, cols)], strip_all.at[col],
            ex_send.at[d], ex_recv.at[d], across(d),
        )
        for d in range(1, cols)
    ]
    own_strip = pltpu.make_async_copy(strip_in.at[col], strip_all.at[col], own_sem.at[2])
    for b in range(blocks):
        factor_block(work, upper, size, NB, b)
        if b == blocks - 2:
            for c in range(cols):
                root = (c * group) % rows

                @pl.when(row == root)
                def _():
                    pltpu.make_async_copy(strip_block(c), strip_in.at[c], copy_sem.at[c]).wait()
                    for d in range(1, rows):
                        strip_copy(c, d).wait_send()

                @pl.when(row != root)
                def _():
                    strip_copy(c, 1).wait_recv()

            own_strip.start()
            for copy in exchange:
                copy.start()
    lower[...] = upper[...].T
    inverse[...] = work[:, size:]
    own_strip.wait()
    for copy in exchange:
        copy.wait()
    full = jnp.concatenate([strip_all[c] for c in range(cols)], axis=1)
    strip[...] = lax.dot_general(
        full, work[:, size:], (((1,), (1,)), ((), ())), precision=HI, preferred_element_type=F32
    )
    own_panel.wait()
    for copy in panels:
        copy.wait()


def split(x):
    high = x.astype(jnp.bfloat16)
    return high, (x - high.astype(F32)).astype(jnp.bfloat16)


def dot_t(a, b):
    dims = (((1,), (1,)), ((), ()))
    (ah, al), (bh, bl) = a, b
    dot = functools.partial(lax.dot_general, dimension_numbers=dims, preferred_element_type=F32)
    return dot(ah, bh) + (dot(ah, bl) + dot(al, bh))


def update_kernel(rows, cols, group, gathered, inverse, strip, slab, panel_out, slab_out):
    row, col = lax.axis_index("prow"), lax.axis_index("pcol")
    block, size = pl.program_id(0), slab.shape[0]
    low = gathered.shape[2]
    full = jnp.concatenate([gathered[c] for c in range(cols)], axis=1)
    factor = dot_t(split(full), split(inverse[...]))
    for c in range(cols):

        @pl.when(col == c)
        def _():
            panel_out[...] = factor[:, c * low : (c + 1) * low]

    product = dot_t(split(factor), split(strip[...]))
    shift = (block * rows + row - col * group) * size
    keep = (
        lax.broadcasted_iota(jnp.int32, slab.shape, 0) + shift
        >= lax.broadcasted_iota(jnp.int32, slab.shape, 1)
    )
    slab_out[...] = jnp.where(keep, slab[...] - product, slab[...])


def local(rows, cols, diag_block, panel, slab):
    high, low = diag_block.shape
    size = high * rows
    local_rows, width = panel.shape
    blocks = local_rows // size
    group = blocks * rows // cols
    any_spec = pl.BlockSpec(memory_space=pl.ANY)
    vmem = pl.BlockSpec(memory_space=pltpu.VMEM)
    dma = pltpu.SemaphoreType.DMA
    square = jax.ShapeDtypeStruct((size, size), F32)
    gathered, lower, inverse, strip = pl.pallas_call(
        functools.partial(gather_kernel, rows, cols, group),
        out_shape=[jax.ShapeDtypeStruct((cols, local_rows, width), F32), square, square, square],
        in_specs=[vmem, any_spec],
        out_specs=[any_spec, vmem, vmem, vmem],
        scratch_shapes=[
            pltpu.VMEM((cols, rows, high, low), F32),
            pltpu.VMEM((size, 2 * size), F32),
            pltpu.VMEM((size, size), F32),
            pltpu.VMEM((cols, size, width), F32),
            pltpu.VMEM((cols, size, width), F32),
            dma((rows,)), dma((rows,)), dma((cols,)), dma((cols,)), dma((3,)),
            dma((cols,)), dma((cols,)), dma((cols, rows)), dma((cols,)),
            dma((cols,)), dma((cols,)), dma((cols,)),
        ],
        compiler_params=pltpu.CompilerParams(collective_id=0, has_side_effects=True),
        name="gather_factor",
    )(diag_block, panel)
    panel_out, slab_out = pl.pallas_call(
        functools.partial(update_kernel, rows, cols, group),
        grid=(blocks,),
        out_shape=[
            jax.ShapeDtypeStruct(panel.shape, F32),
            jax.ShapeDtypeStruct(slab.shape, F32),
        ],
        in_specs=[
            pl.BlockSpec((cols, size, width), lambda i: (0, i, 0)),
            pl.BlockSpec((size, size), lambda i: (0, 0)),
            pl.BlockSpec((size, size), lambda i: (0, 0)),
            pl.BlockSpec((size, slab.shape[1]), lambda i: (i, 0)),
        ],
        out_specs=[
            pl.BlockSpec((size, width), lambda i: (i, 0)),
            pl.BlockSpec((size, slab.shape[1]), lambda i: (i, 0)),
        ],
        name="update",
    )(gathered, inverse, strip, slab)
    diag_out = lax.dynamic_slice(
        lower, (lax.axis_index("prow") * high, lax.axis_index("pcol") * low), (high, low)
    )
    return diag_out, panel_out, slab_out


def solution(mesh):
    spec = P("prow", "pcol")
    return jax.shard_map(
        functools.partial(local, mesh.shape["prow"], mesh.shape["pcol"]),
        mesh=mesh,
        in_specs=(spec, spec, spec),
        out_specs=(spec, spec, spec),
        check_vma=False,
    )
```

```python
import functools

import jax
import jax.numpy as jnp
from jax import lax
from jax.experimental import pallas as pl
from jax.experimental.pallas import tpu as pltpu
from jax.sharding import PartitionSpec as P

HI = lax.Precision.HIGHEST
F32 = jnp.float32
NB = 64


def small(groups, width):
    sub = lax.broadcasted_iota(jnp.int32, (8, 1), 0)
    for j in range(width):
        first, inner = divmod(j, 8)
        row = groups[first][inner : inner + 1, :]
        scale = lax.rsqrt(row[:, j : j + 1])
        row = row * scale
        for g in range(first, width // 8):
            column = groups[g][:, j : j + 1] * scale
            if g == first:
                column = jnp.where(sub > inner, column, 0.0)
                groups[g] = jnp.where(sub == inner, row, groups[g] - column * row)
            else:
                groups[g] = groups[g] - column * row
    return groups


def factor_block(work, upper, size, width, b):
    start, end = b * width, (b + 1) * width
    eye = (
        lax.broadcasted_iota(jnp.int32, (width, width), 0)
        == lax.broadcasted_iota(jnp.int32, (width, width), 1)
    ).astype(F32)
    both = jnp.concatenate([work[start:end, start:end], eye], axis=1)
    groups = small([both[8 * g : 8 * g + 8] for g in range(width // 8)], width)
    inverse = jnp.concatenate(groups, axis=0)[:, width:]
    rows = jnp.dot(inverse, work[start:end, :], precision=HI, preferred_element_type=F32)
    keep = (
        lax.broadcasted_iota(jnp.int32, (width, size), 1)
        >= lax.broadcasted_iota(jnp.int32, (width, size), 0) + start
    )
    left = jnp.where(keep, rows[:, :size], 0.0)
    upper[start:end, :] = left
    work[start:end, size:] = rows[:, size:]
    if end < size:
        column = left.T[end:, :]
        work[end:, :] = work[end:, :] - jnp.dot(
            column,
            jnp.concatenate([left, rows[:, size:]], axis=1),
            precision=HI,
            preferred_element_type=F32,
        )


def gather_kernel(
    rows, cols, group,
    diag, panel,
    gathered, lower, inverse, strip,
    tiles, work, upper, strip_in, strip_all,
    tile_send, tile_recv, wide_send, wide_recv, own_sem,
    panel_send, panel_recv, strip_send, strip_recv, ex_send, ex_recv, copy_sem,
):
    row, col = lax.axis_index("prow"), lax.axis_index("pcol")
    size = upper.shape[0]

    def down(d):
        return {"prow": lax.rem(row + d, rows)}

    def across(d):
        return {"pcol": lax.rem(col + d, cols)}

    def remote(src, dst, send, recv, to):
        return pltpu.make_async_remote_copy(
            src_ref=src, dst_ref=dst, send_sem=send, recv_sem=recv,
            device_id=to, device_id_type=pl.DeviceIdType.MESH,
        )

    barrier = pltpu.get_barrier_semaphore()
    for d in range(1, rows):
        pl.semaphore_signal(barrier, inc=1, device_id=down(d), device_id_type=pl.DeviceIdType.MESH)
    for d in range(1, cols):
        pl.semaphore_signal(barrier, inc=1, device_id=across(d), device_id_type=pl.DeviceIdType.MESH)
    own_tile = pltpu.make_async_copy(diag, tiles.at[col, row], own_sem.at[0])
    own_tile.start()
    own_panel = pltpu.make_async_copy(panel, gathered.at[col], own_sem.at[1])
    own_panel.start()
    pl.semaphore_wait(barrier, rows + cols - 2)

    tile_copies = [
        remote(diag, tiles.at[col, row], tile_send.at[d], tile_recv.at[d], down(d))
        for d in range(1, rows)
    ]
    for copy in tile_copies:
        copy.start()
    own_tile.wait()
    for copy in tile_copies:
        copy.wait()
    wide = [
        remote(tiles.at[col], tiles.at[col], wide_send.at[d], wide_recv.at[d], across(d))
        for d in range(1, cols)
    ]
    for copy in wide:
        copy.start()

    def strip_block(c):
        return panel.at[:, pl.ds((c * group // rows) * size, size)]

    def strip_copy(c, d):
        return remote(
            strip_block(c), strip_in.at[c], strip_send.at[c, d], strip_recv.at[c], down(d)
        )

    for c in range(cols):
        root = (c * group) % rows

        @pl.when(row == root)
        def _():
            pltpu.make_async_copy(strip_block(c), strip_in.at[c], copy_sem.at[c]).start()
            for d in range(1, rows):
                strip_copy(c, d).start()

    for copy in wide:
        copy.wait()
    panels = [
        remote(panel, gathered.at[col], panel_send.at[d], panel_recv.at[d], across(d))
        for d in range(1, cols)
    ]
    for copy in panels:
        copy.start()

    for c in range(cols):
        for r in range(rows):
            high, low = tiles.shape[2], tiles.shape[3]
            work[r * high : (r + 1) * high, c * low : (c + 1) * low] = tiles[c, r]
    work[:, size:] = (
        lax.broadcasted_iota(jnp.int32, (size, size), 0)
        == lax.broadcasted_iota(jnp.int32, (size, size), 1)
    ).astype(F32)

    blocks = size // NB
    exchange = [
        remote(
            strip_in.at[lax.rem(col + d, cols)], strip_all.at[col],
            ex_send.at[d], ex_recv.at[d], across(d),
        )
        for d in range(1, cols)
    ]
    own_strip = pltpu.make_async_copy(strip_in.at[col], strip_all.at[col], own_sem.at[2])
    for b in range(blocks):
        factor_block(work, upper, size, NB, b)
        if b == blocks - 2:
            for c in range(cols):
                root = (c * group) % rows

                @pl.when(row == root)
                def _():
                    pltpu.make_async_copy(strip_block(c), strip_in.at[c], copy_sem.at[c]).wait()
                    for d in range(1, rows):
                        strip_copy(c, d).wait_send()

                @pl.when(row != root)
                def _():
                    strip_copy(c, 1).wait_recv()

            own_strip.start()
            for copy in exchange:
                copy.start()
    lower[...] = upper[...].T
    inverse[...] = work[:, size:]
    own_strip.wait()
    for copy in exchange:
        copy.wait()
    strip[...] = jnp.dot(
        work[:, size:],
        strip_all[...].reshape(size, size),
        precision=HI,
        preferred_element_type=F32,
    )
    own_panel.wait()
    for copy in panels:
        copy.wait()


def split(x):
    high = x.astype(jnp.bfloat16)
    return high, (x - high.astype(F32)).astype(jnp.bfloat16)


def dot_split(a, b):
    (ah, al), (bh, bl) = a, b
    dot = functools.partial(jnp.dot, preferred_element_type=F32)
    return dot(ah, bh) + (dot(ah, bl) + dot(al, bh))


def update_kernel(
    rows, cols, group, gathered, inverse, strip, lower, slab, diag_out, panel_out, slab_out
):
    row, col = lax.axis_index("prow"), lax.axis_index("pcol")
    block, size = pl.program_id(0), slab.shape[0]
    high, low = diag_out.shape

    full = gathered[...].reshape(size, size)
    factor = dot_split(split(inverse[...]), split(full))
    for c in range(cols):

        @pl.when(col == c)
        def _():
            panel_out[...] = factor[c * low : (c + 1) * low, :]

            @pl.when(block == 0)
            def _():
                start = pl.multiple_of(row * high, high)
                diag_out[...] = lower[pl.ds(start, high), c * low : (c + 1) * low]

    product = dot_split(split(factor.T), split(strip[...]))
    shift = (block * rows + row - col * group) * size
    keep = (
        lax.broadcasted_iota(jnp.int32, slab.shape, 0) + shift
        >= lax.broadcasted_iota(jnp.int32, slab.shape, 1)
    )
    slab_out[...] = jnp.where(keep, slab[...] - product, slab[...])


def local(rows, cols, diag_block, panel, slab):
    high, low = diag_block.shape
    size = high * rows
    local_rows, width = panel.shape
    blocks = local_rows // size
    group = blocks * rows // cols
    any_spec = pl.BlockSpec(memory_space=pl.ANY)
    vmem = pl.BlockSpec(memory_space=pltpu.VMEM)
    dma = pltpu.SemaphoreType.DMA
    square = jax.ShapeDtypeStruct((size, size), F32)
    gathered, lower, inverse, strip = pl.pallas_call(
        functools.partial(gather_kernel, rows, cols, group),
        out_shape=[jax.ShapeDtypeStruct((cols, width, local_rows), F32), square, square, square],
        in_specs=[vmem, any_spec],
        out_specs=[any_spec, vmem, vmem, vmem],
        scratch_shapes=[
            pltpu.VMEM((cols, rows, high, low), F32),
            pltpu.VMEM((size, 2 * size), F32),
            pltpu.VMEM((size, size), F32),
            pltpu.VMEM((cols, width, size), F32),
            pltpu.VMEM((cols, width, size), F32),
            dma((rows,)), dma((rows,)), dma((cols,)), dma((cols,)), dma((3,)),
            dma((cols,)), dma((cols,)), dma((cols, rows)), dma((cols,)),
            dma((cols,)), dma((cols,)), dma((cols,)),
        ],
        compiler_params=pltpu.CompilerParams(collective_id=0, has_side_effects=True),
        name="gather_factor",
    )(diag_block, panel.T)
    whole = pl.BlockSpec((size, size), lambda i: (0, 0))
    diag_out, panel_out, slab_out = pl.pallas_call(
        functools.partial(update_kernel, rows, cols, group),
        grid=(blocks,),
        out_shape=[
            jax.ShapeDtypeStruct(diag_block.shape, F32),
            jax.ShapeDtypeStruct((width, local_rows), F32),
            jax.ShapeDtypeStruct(slab.shape, F32),
        ],
        in_specs=[
            pl.BlockSpec((cols, width, size), lambda i: (0, 0, i)),
            whole,
            whole,
            whole,
            pl.BlockSpec((size, slab.shape[1]), lambda i: (i, 0)),
        ],
        out_specs=[
            pl.BlockSpec((high, low), lambda i: (0, 0)),
            pl.BlockSpec((width, size), lambda i: (0, i)),
            pl.BlockSpec((size, slab.shape[1]), lambda i: (i, 0)),
        ],
        name="update",
    )(gathered, inverse, strip, lower, slab)
    return diag_out, panel_out.T, slab_out


def solution(mesh):
    spec = P("prow", "pcol")
    return jax.shard_map(
        functools.partial(local, mesh.shape["prow"], mesh.shape["pcol"]),
        mesh=mesh,
        in_specs=(spec, spec, spec),
        out_specs=(spec, spec, spec),
        check_vma=False,
    )
```

```python
import functools

import jax
import jax.numpy as jnp
from jax import lax
from jax.experimental import pallas as pl
from jax.experimental.pallas import tpu as pltpu
from jax.sharding import PartitionSpec as P

HI = lax.Precision.HIGHEST
F32 = jnp.float32
NB = 64
TILE = 2


def small(groups, width):
    lanes = 2 * width
    sub = lax.broadcasted_iota(jnp.int32, (8, lanes), 0)
    eight = range(8)

    def spread(x):
        return jnp.broadcast_to(x, (8, lanes))

    for g0 in range(width // 8):
        base, first = groups[g0], 8 * g0
        columns = [spread(base[:, first + k : first + k + 1]) for k in eight]
        d = {(m, k): spread(columns[k][m : m + 1, :]) for k in eight for m in range(k, 8)}
        rows = [spread(base[k : k + 1, :]) for k in eight]
        scales = []
        for k in eight:
            scale = lax.rsqrt(d[k, k])
            scales.append(scale)
            for m in range(k + 1, 8):
                d[m, k] = d[m, k] * scale
            for m in range(k + 1, 8):
                for q in range(k + 1, m + 1):
                    d[m, q] = d[m, q] - d[m, k] * d[q, k]
            rows[k] = rows[k] * scale
            for m in range(k + 1, 8):
                rows[m] = rows[m] - d[m, k] * rows[k]
        back = [None] * 8
        for k in reversed(eight):
            total = rows[k]
            for m in range(k + 1, 8):
                total = total - d[m, k] * back[m]
            back[k] = total * scales[k]
        solved = rows[0]
        for k in range(1, 8):
            solved = jnp.where(sub == k, rows[k], solved)
        groups[g0] = solved
        for g in range(g0 + 1, width // 8):
            terms = [spread(groups[g][:, first + k : first + k + 1]) * back[k] for k in eight]
            while len(terms) > 1:
                terms = [x + y for x, y in zip(terms[::2], terms[1::2])]
            groups[g] = groups[g] - terms[0]
    return groups


def factor_block(work, upper, size, width, b):
    start, end = b * width, (b + 1) * width
    eye = (
        lax.broadcasted_iota(jnp.int32, (width, width), 0)
        == lax.broadcasted_iota(jnp.int32, (width, width), 1)
    ).astype(F32)
    both = jnp.concatenate([work[start:end, start:end], eye], axis=1)
    groups = small([both[8 * g : 8 * g + 8] for g in range(width // 8)], width)
    inverse = jnp.concatenate(groups, axis=0)[:, width:]
    rows = jnp.dot(inverse, work[start:end, :], precision=HI, preferred_element_type=F32)
    keep = (
        lax.broadcasted_iota(jnp.int32, (width, size), 1)
        >= lax.broadcasted_iota(jnp.int32, (width, size), 0) + start
    )
    left = jnp.where(keep, rows[:, :size], 0.0)
    upper[start:end, :] = left
    work[start:end, size:] = rows[:, size:]
    if end < size:
        column = left.T[end:, :]
        work[end:, :] = work[end:, :] - jnp.dot(
            column,
            jnp.concatenate([left, rows[:, size:]], axis=1),
            precision=HI,
            preferred_element_type=F32,
        )


def gather_kernel(
    rows, cols, group,
    diag, panel,
    gathered, lower, inverse, strip,
    tiles, work, upper, strip_in, strip_all,
    tile_send, tile_recv, wide_send, wide_recv, own_sem,
    panel_send, panel_recv, strip_send, strip_recv, ex_send, ex_recv, copy_sem,
):
    row, col = lax.axis_index("prow"), lax.axis_index("pcol")
    size = upper.shape[0]
    piece = panel.shape[1] // 4

    def down(d):
        return {"prow": lax.rem(row + d, rows)}

    def across(d):
        return {"pcol": lax.rem(col + d, cols)}

    def remote(src, dst, send, recv, to):
        return pltpu.make_async_remote_copy(
            src_ref=src, dst_ref=dst, send_sem=send, recv_sem=recv,
            device_id=to, device_id_type=pl.DeviceIdType.MESH,
        )

    barrier = pltpu.get_barrier_semaphore()
    for d in range(1, rows):
        pl.semaphore_signal(barrier, inc=1, device_id=down(d), device_id_type=pl.DeviceIdType.MESH)
    for d in range(1, cols):
        pl.semaphore_signal(barrier, inc=1, device_id=across(d), device_id_type=pl.DeviceIdType.MESH)
    own_tile = pltpu.make_async_copy(diag, tiles.at[col, row], own_sem.at[0])
    own_tile.start()
    own_panel = pltpu.make_async_copy(panel, gathered.at[col], own_sem.at[1])
    own_panel.start()
    pl.semaphore_wait(barrier, rows + cols - 2)

    tile_copies = [
        remote(diag, tiles.at[col, row], tile_send.at[d], tile_recv.at[d], down(d))
        for d in range(1, rows)
    ]
    for copy in tile_copies:
        copy.start()

    def part(i):
        return pl.ds(i * piece, piece)

    def piece_copy(i, d, to):
        return remote(
            panel.at[:, part(i)], gathered.at[col, :, part(i)],
            panel_send.at[d, i], panel_recv.at[d, i], to,
        )

    relay = cols == 4
    forwards = []
    if relay:
        side, other = col + 1 - 2 * lax.rem(col, 2), lax.rem(col + 2, 4)
        to_side, to_other = {"pcol": side}, {"pcol": other}
        early = [piece_copy(0, 0, to_side), piece_copy(2, 1, to_other)]
        late = []
        for i in range(1, 4):
            late += [piece_copy(i, 0, to_side), piece_copy((i + 2) % 4, 1, to_other)]
        lower_half, upper_half = pl.ds(0, 2 * piece), pl.ds(2 * piece, 2 * piece)
        for slot, (source, half, to) in enumerate(
            [(side, lower_half, to_other), (other, upper_half, to_side)]
        ):
            view = gathered.at[source, :, half]
            forwards.append(remote(view, view, panel_send.at[2, slot], panel_recv.at[2, slot], to))
    else:
        early = []
        late = [piece_copy(i, d, across(d)) for d in range(1, cols) for i in range(4)]
    for copy in early:
        copy.start()

    def strip_block(c):
        return panel.at[:, pl.ds((c * group // rows) * size, size)]

    def strip_sends(c, src):
        root = (c * group) % rows
        place, origin, last = row // 2, root // 2, rows // 2 - 1
        spine = lax.rem(row, 2) == root % 2
        steps = [
            (spine & (place >= origin) & (place < last), 2),
            (spine & (place <= origin) & (place > 0), -2),
            (spine, 1 - 2 * (root % 2)),
        ]
        return [
            (
                cond,
                remote(
                    src, strip_in.at[c], strip_send.at[c, i], strip_recv.at[c],
                    {"prow": lax.rem(row + step + rows, rows)},
                ),
            )
            for i, (cond, step) in enumerate(steps)
        ]

    def strip_start(c, src):
        for cond, copy in strip_sends(c, src):
            pl.when(cond)(copy.start)

    def strip_own(c):
        return pltpu.make_async_copy(strip_block(c), strip_in.at[c], copy_sem.at[c])

    for c in range(cols):
        root = (c * group) % rows

        @pl.when(row == root)
        def _():
            strip_own(c).start()
            strip_start(c, strip_block(c))

    own_tile.wait()
    for copy in tile_copies:
        copy.wait()
    wide = [
        remote(tiles.at[col], tiles.at[col], wide_send.at[d], wide_recv.at[d], across(d))
        for d in range(1, cols)
    ]
    for copy in wide:
        copy.start()
    for copy in late:
        copy.start()

    for c in range(cols):
        root = (c * group) % rows

        @pl.when((row != root) & (lax.rem(row, 2) == root % 2))
        def _():
            strip_sends(c, strip_in.at[c])[2][1].wait_recv()
            strip_start(c, strip_in.at[c])

    for copy in wide:
        copy.wait()

    for c in range(cols):
        for r in range(rows):
            high, low = tiles.shape[2], tiles.shape[3]
            work[r * high : (r + 1) * high, c * low : (c + 1) * low] = tiles[c, r]
    work[:, size:] = (
        lax.broadcasted_iota(jnp.int32, (size, size), 0)
        == lax.broadcasted_iota(jnp.int32, (size, size), 1)
    ).astype(F32)

    blocks = size // NB
    exchange = [
        remote(
            strip_in.at[lax.rem(col + d, cols)], strip_all.at[col],
            ex_send.at[d], ex_recv.at[d], across(d),
        )
        for d in range(1, cols)
    ]
    own_strip = pltpu.make_async_copy(strip_in.at[col], strip_all.at[col], own_sem.at[2])
    for b in range(blocks):
        factor_block(work, upper, size, NB, b)
        if b == 0:
            for c in range(cols):
                root = (c * group) % rows

                @pl.when(row == root)
                def _():
                    strip_own(c).wait()

                @pl.when(lax.rem(row, 2) != root % 2)
                def _():
                    strip_sends(c, strip_in.at[c])[2][1].wait_recv()

            own_strip.start()
            for copy in exchange:
                copy.start()
            if relay:
                for copy in (early[0], late[0], early[1], late[1]):
                    copy.wait_recv()
                for copy in forwards:
                    copy.start()
    lower[...] = upper[...].T
    inverse[...] = work[:, size:]
    own_strip.wait()
    for copy in exchange:
        copy.wait()
    strip[...] = jnp.dot(
        work[:, size:],
        strip_all[...].reshape(size, size),
        precision=HI,
        preferred_element_type=F32,
    )
    for c in range(cols):
        for cond, copy in strip_sends(c, strip_in.at[c]):
            pl.when(cond)(copy.wait_send)
    own_panel.wait()
    for copy in early + late:
        copy.wait_send()
    for copy in late[2:] if relay else late:
        copy.wait_recv()
    for copy in forwards:
        copy.wait()


def split(x):
    high = x.astype(jnp.bfloat16)
    return high, (x - high.astype(F32)).astype(jnp.bfloat16)


def dot_split(a, b):
    (ah, al), (bh, bl) = a, b
    dot = functools.partial(jnp.dot, preferred_element_type=F32)
    return dot(ah, bh) + (dot(ah, bl) + dot(al, bh))


def update_kernel(
    rows, cols, group, gathered, inverse, strip, lower, slab, diag_out, panel_out, slab_out,
    inv_high, inv_low, strip_high, strip_low,
):
    row, col = lax.axis_index("prow"), lax.axis_index("pcol")
    step, size = pl.program_id(0), strip.shape[0]
    high, low = diag_out.shape
    count = slab.shape[0] // size

    @pl.when(step == 0)
    def _():
        inv_high[...], inv_low[...] = split(inverse[...])
        strip_high[...], strip_low[...] = split(strip[...])

    full = gathered[...].reshape(size, count * size)
    factor = dot_split((inv_high[...], inv_low[...]), split(full))
    for c in range(cols):

        @pl.when(col == c)
        def _():
            panel_out[...] = factor[c * low : (c + 1) * low, :]

            @pl.when(step == 0)
            def _():
                start = pl.multiple_of(row * high, high)
                diag_out[...] = lower[pl.ds(start, high), c * low : (c + 1) * low]

    product = dot_split(split(factor.T), (strip_high[...], strip_low[...]))
    for i in range(count):
        here = slice(i * size, (i + 1) * size)
        shift = ((step * count + i) * rows + row - col * group) * size
        shape = (size, slab.shape[1])
        keep = (
            lax.broadcasted_iota(jnp.int32, shape, 0) + shift
            >= lax.broadcasted_iota(jnp.int32, shape, 1)
        )
        slab_out[here, :] = jnp.where(keep, slab[here, :] - product[here, :], slab[here, :])


def local(rows, cols, diag_block, panel, slab):
    high, low = diag_block.shape
    size = high * rows
    local_rows, width = panel.shape
    blocks = local_rows // size
    group = blocks * rows // cols
    any_spec = pl.BlockSpec(memory_space=pl.ANY)
    vmem = pl.BlockSpec(memory_space=pltpu.VMEM)
    dma = pltpu.SemaphoreType.DMA
    square = jax.ShapeDtypeStruct((size, size), F32)
    gathered, lower, inverse, strip = pl.pallas_call(
        functools.partial(gather_kernel, rows, cols, group),
        out_shape=[jax.ShapeDtypeStruct((cols, width, local_rows), F32), square, square, square],
        in_specs=[vmem, any_spec],
        out_specs=[any_spec, vmem, vmem, vmem],
        scratch_shapes=[
            pltpu.VMEM((cols, rows, high, low), F32),
            pltpu.VMEM((size, 2 * size), F32),
            pltpu.VMEM((size, size), F32),
            pltpu.VMEM((cols, width, size), F32),
            pltpu.VMEM((cols, width, size), F32),
            dma((rows,)), dma((rows,)), dma((cols,)), dma((cols,)), dma((3,)),
            dma((cols, 4)), dma((cols, 4)), dma((cols, 3)), dma((cols,)),
            dma((cols,)), dma((cols,)), dma((cols,)),
        ],
        compiler_params=pltpu.CompilerParams(collective_id=0, has_side_effects=True),
        name="gather_factor",
    )(diag_block, panel.T)
    tile = TILE if blocks % TILE == 0 else 1
    whole = pl.BlockSpec((size, size), lambda i: (0, 0))
    diag_out, panel_out, slab_out = pl.pallas_call(
        functools.partial(update_kernel, rows, cols, group),
        grid=(blocks // tile,),
        out_shape=[
            jax.ShapeDtypeStruct(diag_block.shape, F32),
            jax.ShapeDtypeStruct((width, local_rows), F32),
            jax.ShapeDtypeStruct(slab.shape, F32),
        ],
        in_specs=[
            pl.BlockSpec((cols, width, tile * size), lambda i: (0, 0, i)),
            whole,
            whole,
            whole,
            pl.BlockSpec((tile * size, slab.shape[1]), lambda i: (i, 0)),
        ],
        out_specs=[
            pl.BlockSpec((high, low), lambda i: (0, 0)),
            pl.BlockSpec((width, tile * size), lambda i: (0, i)),
            pl.BlockSpec((tile * size, slab.shape[1]), lambda i: (i, 0)),
        ],
        scratch_shapes=[pltpu.VMEM((size, size), jnp.bfloat16)] * 4,
        name="update",
    )(gathered, inverse, strip, lower, slab)
    return diag_out, panel_out.T, slab_out


def solution(mesh):
    spec = P("prow", "pcol")
    return jax.shard_map(
        functools.partial(local, mesh.shape["prow"], mesh.shape["pcol"]),
        mesh=mesh,
        in_specs=(spec, spec, spec),
        out_specs=(spec, spec, spec),
        check_vma=False,
    )
```

```python
import functools

import jax
import jax.numpy as jnp
from jax import lax
from jax.experimental import pallas as pl
from jax.experimental.pallas import tpu as pltpu
from jax.sharding import PartitionSpec as P

HI = lax.Precision.HIGHEST
F32 = jnp.float32
NB = 64
TILE = 4


def small(groups, width):
    lanes = 2 * width
    sub = lax.broadcasted_iota(jnp.int32, (8, lanes), 0)
    eight = range(8)

    def spread(x):
        return jnp.broadcast_to(x, (8, lanes))

    for g0 in range(width // 8):
        base, first = groups[g0], 8 * g0
        columns = [spread(base[:, first + k : first + k + 1]) for k in eight]
        d = {(m, k): spread(columns[k][m : m + 1, :]) for k in eight for m in range(k, 8)}
        rows = [spread(base[k : k + 1, :]) for k in eight]
        scales = []
        for k in eight:
            scale = lax.rsqrt(d[k, k])
            scales.append(scale)
            for m in range(k + 1, 8):
                d[m, k] = d[m, k] * scale
            for m in range(k + 1, 8):
                for q in range(k + 1, m + 1):
                    d[m, q] = d[m, q] - d[m, k] * d[q, k]
            rows[k] = rows[k] * scale
            for m in range(k + 1, 8):
                rows[m] = rows[m] - d[m, k] * rows[k]
        back = [None] * 8
        for k in reversed(eight):
            total = rows[k]
            for m in range(k + 1, 8):
                total = total - d[m, k] * back[m]
            back[k] = total * scales[k]
        solved = rows[0]
        for k in range(1, 8):
            solved = jnp.where(sub == k, rows[k], solved)
        groups[g0] = solved
        for g in range(g0 + 1, width // 8):
            terms = [spread(groups[g][:, first + k : first + k + 1]) * back[k] for k in eight]
            while len(terms) > 1:
                terms = [x + y for x, y in zip(terms[::2], terms[1::2])]
            groups[g] = groups[g] - terms[0]
    return groups


def factor_block(work, upper, size, width, b):
    start, end = b * width, (b + 1) * width
    eye = (
        lax.broadcasted_iota(jnp.int32, (width, width), 0)
        == lax.broadcasted_iota(jnp.int32, (width, width), 1)
    ).astype(F32)
    both = jnp.concatenate([work[start:end, start:end], eye], axis=1)
    groups = small([both[8 * g : 8 * g + 8] for g in range(width // 8)], width)
    inverse = jnp.concatenate(groups, axis=0)[:, width:]
    rows = jnp.dot(inverse, work[start:end, :], precision=HI, preferred_element_type=F32)
    keep = (
        lax.broadcasted_iota(jnp.int32, (width, size), 1)
        >= lax.broadcasted_iota(jnp.int32, (width, size), 0) + start
    )
    left = jnp.where(keep, rows[:, :size], 0.0)
    upper[start:end, :] = left
    work[start:end, size:] = rows[:, size:]
    if end < size:
        column = left.T[end:, :]
        work[end:, :] = work[end:, :] - jnp.dot(
            column,
            jnp.concatenate([left, rows[:, size:]], axis=1),
            precision=HI,
            preferred_element_type=F32,
        )


def gather_kernel(
    rows, cols, group,
    diag, panel,
    gathered, lower, inverse, strip,
    tiles, work, upper, strip_in, strip_all,
    tile_send, tile_recv, wide_send, wide_recv, own_sem,
    panel_send, panel_recv, strip_send, strip_recv, ex_send, ex_recv, copy_sem,
):
    row, col = lax.axis_index("prow"), lax.axis_index("pcol")
    size = upper.shape[0]
    piece = panel.shape[1] // 4

    def down(d):
        return {"prow": lax.rem(row + d, rows)}

    def across(d):
        return {"pcol": lax.rem(col + d, cols)}

    def remote(src, dst, send, recv, to):
        return pltpu.make_async_remote_copy(
            src_ref=src, dst_ref=dst, send_sem=send, recv_sem=recv,
            device_id=to, device_id_type=pl.DeviceIdType.MESH,
        )

    barrier = pltpu.get_barrier_semaphore()
    for d in range(1, rows):
        pl.semaphore_signal(barrier, inc=1, device_id=down(d), device_id_type=pl.DeviceIdType.MESH)
    for d in range(1, cols):
        pl.semaphore_signal(barrier, inc=1, device_id=across(d), device_id_type=pl.DeviceIdType.MESH)
    own_tile = pltpu.make_async_copy(diag, tiles.at[col, row], own_sem.at[0])
    own_tile.start()
    own_panel = pltpu.make_async_copy(panel, gathered.at[col], own_sem.at[1])
    own_panel.start()
    pl.semaphore_wait(barrier, rows + cols - 2)

    tile_copies = [
        remote(diag, tiles.at[col, row], tile_send.at[d], tile_recv.at[d], down(d))
        for d in range(1, rows)
    ]
    for copy in tile_copies:
        copy.start()

    def part(i):
        return pl.ds(i * piece, piece)

    def piece_copy(i, d, to):
        return remote(
            panel.at[:, part(i)], gathered.at[col, :, part(i)],
            panel_send.at[d, i], panel_recv.at[d, i], to,
        )

    relay = cols == 4
    forwards = []
    if relay:
        side, other = col + 1 - 2 * lax.rem(col, 2), lax.rem(col + 2, 4)
        to_side, to_other = {"pcol": side}, {"pcol": other}
        early = [piece_copy(0, 0, to_side), piece_copy(2, 1, to_other)]
        late = []
        for i in range(1, 4):
            late += [piece_copy(i, 0, to_side), piece_copy((i + 2) % 4, 1, to_other)]
        lower_half, upper_half = pl.ds(0, 2 * piece), pl.ds(2 * piece, 2 * piece)
        for slot, (source, half, to) in enumerate(
            [(side, lower_half, to_other), (other, upper_half, to_side)]
        ):
            view = gathered.at[source, :, half]
            forwards.append(remote(view, view, panel_send.at[2, slot], panel_recv.at[2, slot], to))
    else:
        early = []
        late = [piece_copy(i, d, across(d)) for d in range(1, cols) for i in range(4)]
    for copy in early:
        copy.start()

    def strip_block(c):
        return panel.at[:, pl.ds((c * group // rows) * size, size)]

    def strip_sends(c, src):
        root = (c * group) % rows
        place, origin, last = row // 2, root // 2, rows // 2 - 1
        spine = lax.rem(row, 2) == root % 2
        steps = [
            (spine & (place >= origin) & (place < last), 2),
            (spine & (place <= origin) & (place > 0), -2),
            (spine, 1 - 2 * (root % 2)),
        ]
        return [
            (
                cond,
                remote(
                    src, strip_in.at[c], strip_send.at[c, i], strip_recv.at[c],
                    {"prow": lax.rem(row + step + rows, rows)},
                ),
            )
            for i, (cond, step) in enumerate(steps)
        ]

    def strip_start(c, src):
        for cond, copy in strip_sends(c, src):
            pl.when(cond)(copy.start)

    def strip_own(c):
        return pltpu.make_async_copy(strip_block(c), strip_in.at[c], copy_sem.at[c])

    for c in range(cols):
        root = (c * group) % rows

        @pl.when(row == root)
        def _():
            strip_own(c).start()
            strip_start(c, strip_block(c))

    own_tile.wait()
    for copy in tile_copies:
        copy.wait()
    wide = [
        remote(tiles.at[col], tiles.at[col], wide_send.at[d], wide_recv.at[d], across(d))
        for d in range(1, cols)
    ]
    for copy in wide:
        copy.start()
    for copy in late:
        copy.start()

    for c in range(cols):
        root = (c * group) % rows

        @pl.when((row != root) & (lax.rem(row, 2) == root % 2))
        def _():
            strip_sends(c, strip_in.at[c])[2][1].wait_recv()
            strip_start(c, strip_in.at[c])

    for copy in wide:
        copy.wait()

    for c in range(cols):
        for r in range(rows):
            high, low = tiles.shape[2], tiles.shape[3]
            work[r * high : (r + 1) * high, c * low : (c + 1) * low] = tiles[c, r]
    work[:, size:] = (
        lax.broadcasted_iota(jnp.int32, (size, size), 0)
        == lax.broadcasted_iota(jnp.int32, (size, size), 1)
    ).astype(F32)

    blocks = size // NB
    exchange = [
        remote(
            strip_in.at[lax.rem(col + d, cols)], strip_all.at[col],
            ex_send.at[d], ex_recv.at[d], across(d),
        )
        for d in range(1, cols)
    ]
    own_strip = pltpu.make_async_copy(strip_in.at[col], strip_all.at[col], own_sem.at[2])
    for b in range(blocks):
        factor_block(work, upper, size, NB, b)
        if b == 0:
            for c in range(cols):
                root = (c * group) % rows

                @pl.when(row == root)
                def _():
                    strip_own(c).wait()

                @pl.when(lax.rem(row, 2) != root % 2)
                def _():
                    strip_sends(c, strip_in.at[c])[2][1].wait_recv()

            own_strip.start()
            for copy in exchange:
                copy.start()
            if relay:
                for copy in (early[0], late[0], early[1], late[1]):
                    copy.wait_recv()
                for copy in forwards:
                    copy.start()
    lower[...] = upper[...].T
    inverse[...] = work[:, size:]
    own_strip.wait()
    for copy in exchange:
        copy.wait()
    strip[...] = jnp.dot(
        work[:, size:],
        strip_all[...].reshape(size, size),
        precision=HI,
        preferred_element_type=F32,
    )
    for c in range(cols):
        for cond, copy in strip_sends(c, strip_in.at[c]):
            pl.when(cond)(copy.wait_send)
    own_panel.wait()
    for copy in early + late:
        copy.wait_send()
    for copy in late[2:] if relay else late:
        copy.wait_recv()
    for copy in forwards:
        copy.wait()


def split(x):
    high = x.astype(jnp.bfloat16)
    return high, (x - high.astype(F32)).astype(jnp.bfloat16)


def dot_split(a, b):
    (ah, al), (bh, bl) = a, b
    dot = functools.partial(jnp.dot, preferred_element_type=F32)
    return dot(ah, bh) + (dot(ah, bl) + dot(al, bh))


def update_kernel(
    rows, cols, group, gathered, inverse, strip, lower, slab, diag_out, panel_out, slab_out,
    inv_high, inv_low, strip_high, strip_low,
):
    row, col = lax.axis_index("prow"), lax.axis_index("pcol")
    step, size = pl.program_id(0), strip.shape[0]
    high, low = diag_out.shape
    count = slab.shape[0] // size

    @pl.when(step == 0)
    def _():
        inv_high[...], inv_low[...] = split(inverse[...])
        strip_high[...], strip_low[...] = split(strip[...])

    full = gathered[...].reshape(size, count * size)
    factor = dot_split((inv_high[...], inv_low[...]), split(full))
    for c in range(cols):

        @pl.when(col == c)
        def _():
            panel_out[...] = factor[c * low : (c + 1) * low, :]

            @pl.when(step == 0)
            def _():
                start = pl.multiple_of(row * high, high)
                diag_out[...] = lower[pl.ds(start, high), c * low : (c + 1) * low]

    product = dot_split(split(factor.T), (strip_high[...], strip_low[...]))
    for i in range(count):
        here = slice(i * size, (i + 1) * size)
        shift = ((step * count + i) * rows + row - col * group) * size
        shape = (size, slab.shape[1])
        keep = (
            lax.broadcasted_iota(jnp.int32, shape, 0) + shift
            >= lax.broadcasted_iota(jnp.int32, shape, 1)
        )
        slab_out[here, :] = jnp.where(keep, slab[here, :] - product[here, :], slab[here, :])


def local(rows, cols, diag_block, panel, slab):
    high, low = diag_block.shape
    size = high * rows
    local_rows, width = panel.shape
    blocks = local_rows // size
    group = blocks * rows // cols
    any_spec = pl.BlockSpec(memory_space=pl.ANY)
    vmem = pl.BlockSpec(memory_space=pltpu.VMEM)
    dma = pltpu.SemaphoreType.DMA
    square = jax.ShapeDtypeStruct((size, size), F32)
    gathered, lower, inverse, strip = pl.pallas_call(
        functools.partial(gather_kernel, rows, cols, group),
        out_shape=[jax.ShapeDtypeStruct((cols, width, local_rows), F32), square, square, square],
        in_specs=[vmem, any_spec],
        out_specs=[any_spec, vmem, vmem, vmem],
        scratch_shapes=[
            pltpu.VMEM((cols, rows, high, low), F32),
            pltpu.VMEM((size, 2 * size), F32),
            pltpu.VMEM((size, size), F32),
            pltpu.VMEM((cols, width, size), F32),
            pltpu.VMEM((cols, width, size), F32),
            dma((rows,)), dma((rows,)), dma((cols,)), dma((cols,)), dma((3,)),
            dma((cols, 4)), dma((cols, 4)), dma((cols, 3)), dma((cols,)),
            dma((cols,)), dma((cols,)), dma((cols,)),
        ],
        compiler_params=pltpu.CompilerParams(collective_id=0, has_side_effects=True),
        name="gather_factor",
    )(diag_block, panel.T)
    tile = TILE if blocks % TILE == 0 else 1
    whole = pl.BlockSpec((size, size), lambda i: (0, 0))
    diag_out, panel_out, slab_out = pl.pallas_call(
        functools.partial(update_kernel, rows, cols, group),
        grid=(blocks // tile,),
        out_shape=[
            jax.ShapeDtypeStruct(diag_block.shape, F32),
            jax.ShapeDtypeStruct((width, local_rows), F32),
            jax.ShapeDtypeStruct(slab.shape, F32),
        ],
        in_specs=[
            pl.BlockSpec((cols, width, tile * size), lambda i: (0, 0, i)),
            whole,
            whole,
            whole,
            pl.BlockSpec((tile * size, slab.shape[1]), lambda i: (i, 0)),
        ],
        out_specs=[
            pl.BlockSpec((high, low), lambda i: (0, 0)),
            pl.BlockSpec((width, tile * size), lambda i: (0, i)),
            pl.BlockSpec((tile * size, slab.shape[1]), lambda i: (i, 0)),
        ],
        scratch_shapes=[pltpu.VMEM((size, size), jnp.bfloat16)] * 4,
        name="update",
    )(gathered, inverse, strip, lower, slab)
    return diag_out, panel_out.T, slab_out


def solution(mesh):
    spec = P("prow", "pcol")
    return jax.shard_map(
        functools.partial(local, mesh.shape["prow"], mesh.shape["pcol"]),
        mesh=mesh,
        in_specs=(spec, spec, spec),
        out_specs=(spec, spec, spec),
        check_vma=False,
    )
```

```python
import functools

import jax
import jax.numpy as jnp
from jax import lax
from jax.experimental import pallas as pl
from jax.experimental.pallas import tpu as pltpu
from jax.sharding import PartitionSpec as P

HI = lax.Precision.HIGHEST
F32 = jnp.float32
NB = 64
TILE = 4


def small(groups, width):
    lanes = 2 * width
    sub = lax.broadcasted_iota(jnp.int32, (8, lanes), 0)
    eight = range(8)

    def spread(x):
        return jnp.broadcast_to(x, (8, lanes))

    for g0 in range(width // 8):
        base, first = groups[g0], 8 * g0
        columns = [spread(base[:, first + k : first + k + 1]) for k in eight]
        d = {(m, k): spread(columns[k][m : m + 1, :]) for k in eight for m in range(k, 8)}
        rows = [spread(base[k : k + 1, :]) for k in eight]
        scales = []
        for k in eight:
            scale = lax.rsqrt(d[k, k])
            scales.append(scale)
            for m in range(k + 1, 8):
                d[m, k] = d[m, k] * scale
            for m in range(k + 1, 8):
                for q in range(k + 1, m + 1):
                    d[m, q] = d[m, q] - d[m, k] * d[q, k]
            rows[k] = rows[k] * scale
            for m in range(k + 1, 8):
                rows[m] = rows[m] - d[m, k] * rows[k]
        back = [None] * 8
        for k in reversed(eight):
            total = rows[k]
            for m in range(k + 1, 8):
                total = total - d[m, k] * back[m]
            back[k] = total * scales[k]
        solved = rows[0]
        for k in range(1, 8):
            solved = jnp.where(sub == k, rows[k], solved)
        groups[g0] = solved
        for g in range(g0 + 1, width // 8):
            terms = [spread(groups[g][:, first + k : first + k + 1]) * back[k] for k in eight]
            while len(terms) > 1:
                terms = [x + y for x, y in zip(terms[::2], terms[1::2])]
            groups[g] = groups[g] - terms[0]
    return groups


def factor_block(work, upper, size, width, b):
    start, end = b * width, (b + 1) * width
    eye = (
        lax.broadcasted_iota(jnp.int32, (width, width), 0)
        == lax.broadcasted_iota(jnp.int32, (width, width), 1)
    ).astype(F32)
    both = jnp.concatenate([work[start:end, start:end], eye], axis=1)
    groups = small([both[8 * g : 8 * g + 8] for g in range(width // 8)], width)
    inverse = jnp.concatenate(groups, axis=0)[:, width:]
    rows = jnp.dot(inverse, work[start:end, :], precision=HI, preferred_element_type=F32)
    keep = (
        lax.broadcasted_iota(jnp.int32, (width, size), 1)
        >= lax.broadcasted_iota(jnp.int32, (width, size), 0) + start
    )
    left = jnp.where(keep, rows[:, :size], 0.0)
    upper[start:end, :] = left
    work[start:end, size:] = rows[:, size:]
    if end < size:
        column = left.T[end:, :]
        work[end:, :] = work[end:, :] - jnp.dot(
            column,
            jnp.concatenate([left, rows[:, size:]], axis=1),
            precision=HI,
            preferred_element_type=F32,
        )


def gather_kernel(
    rows, cols, group,
    diag, panel,
    gathered, lower, inverse, strip,
    tiles, work, upper, strip_all,
    tile_send, tile_recv, wide_send, wide_recv, own_sem,
    panel_send, panel_recv, strip_send, strip_recv, ex_send, ex_recv, copy_sem,
):
    row, col = lax.axis_index("prow"), lax.axis_index("pcol")
    size = upper.shape[0]
    piece = panel.shape[1] // 4

    def down(d):
        return {"prow": lax.rem(row + d, rows)}

    def across(d):
        return {"pcol": lax.rem(col + d, cols)}

    def remote(src, dst, send, recv, to):
        return pltpu.make_async_remote_copy(
            src_ref=src, dst_ref=dst, send_sem=send, recv_sem=recv,
            device_id=to, device_id_type=pl.DeviceIdType.MESH,
        )

    barrier = pltpu.get_barrier_semaphore()
    for d in range(1, rows):
        pl.semaphore_signal(barrier, inc=1, device_id=down(d), device_id_type=pl.DeviceIdType.MESH)
    for d in range(1, cols):
        pl.semaphore_signal(barrier, inc=1, device_id=across(d), device_id_type=pl.DeviceIdType.MESH)
    own_tile = pltpu.make_async_copy(diag, tiles.at[col, row], own_sem.at[0])
    own_tile.start()
    own_panel = pltpu.make_async_copy(panel, gathered.at[col], own_sem.at[1])
    own_panel.start()
    pl.semaphore_wait(barrier, rows + cols - 2)

    tile_copies = [
        remote(diag, tiles.at[col, row], tile_send.at[d], tile_recv.at[d], down(d))
        for d in range(1, rows)
    ]
    for copy in tile_copies:
        copy.start()

    def part(i):
        return pl.ds(i * piece, piece)

    def piece_copy(i, d, to):
        return remote(
            panel.at[:, part(i)], gathered.at[col, :, part(i)],
            panel_send.at[d, i], panel_recv.at[d, i], to,
        )

    relay = cols == 4
    forwards = []
    if relay:
        side, other = col + 1 - 2 * lax.rem(col, 2), lax.rem(col + 2, 4)
        to_side, to_other = {"pcol": side}, {"pcol": other}
        early = [piece_copy(0, 0, to_side), piece_copy(2, 1, to_other)]
        late = []
        for i in range(1, 4):
            late += [piece_copy(i, 0, to_side), piece_copy((i + 2) % 4, 1, to_other)]
        lower_half, upper_half = pl.ds(0, 2 * piece), pl.ds(2 * piece, 2 * piece)
        for slot, (source, half, to) in enumerate(
            [(side, lower_half, to_other), (other, upper_half, to_side)]
        ):
            view = gathered.at[source, :, half]
            forwards.append(remote(view, view, panel_send.at[2, slot], panel_recv.at[2, slot], to))
    else:
        early = []
        late = [piece_copy(i, d, across(d)) for d in range(1, cols) for i in range(4)]
    my_root = lax.rem(col * group, rows)
    place, origin, last = row // 2, my_root // 2, rows // 2 - 1
    spine = lax.rem(row, 2) == lax.rem(my_root, 2)
    steps = [
        (spine & (place >= origin) & (place < last), 2),
        (spine & (place <= origin) & (place > 0), -2),
        (spine, 1 - 2 * lax.rem(my_root, 2)),
    ]

    def strip_block(c):
        start = pl.multiple_of(c * group // rows * size, size)
        return panel.at[:, pl.ds(start, size)]

    def strip_give(c):
        give = (row == (c * group) % rows) & (col != c)
        return give, remote(
            strip_block(c), strip_all.at[col], ex_send.at[c], ex_recv.at[col], {"pcol": c}
        )

    def strip_take(c):
        return remote(
            strip_block(c), strip_all.at[c], ex_send.at[c], ex_recv.at[c], {"pcol": lax.rem(col + 1, cols)}
        )

    def strip_sends(c):
        view = strip_all.at[c]
        return [
            (
                cond,
                remote(
                    view, view, strip_send.at[c, i], strip_recv.at[c],
                    {"prow": lax.rem(row + step + rows, rows)},
                ),
            )
            for i, (cond, step) in enumerate(steps)
        ]

    def strip_start(c):
        for cond, copy in strip_sends(c):
            pl.when(cond)(copy.start)

    for c in range(cols):
        give, copy = strip_give(c)
        pl.when(give)(copy.start)
    for copy in early:
        copy.start()

    @pl.when(row == my_root)
    def _():
        own = pltpu.make_async_copy(strip_block(col), strip_all.at[col], copy_sem.at[0])
        own.start()
        own.wait()
        for c in range(cols):
            pl.when(col != c)(strip_take(c).wait_recv)
            strip_start(c)

    own_tile.wait()
    for copy in tile_copies:
        copy.wait()
    wide = [
        remote(tiles.at[col], tiles.at[col], wide_send.at[d], wide_recv.at[d], across(d))
        for d in range(1, cols)
    ]
    for copy in wide:
        copy.start()
    for copy in late:
        copy.start()

    @pl.when((row != my_root) & spine)
    def _():
        for c in range(cols):
            strip_sends(c)[2][1].wait_recv()
            strip_start(c)

    for copy in wide:
        copy.wait()

    for c in range(cols):
        for r in range(rows):
            high, low = tiles.shape[2], tiles.shape[3]
            work[r * high : (r + 1) * high, c * low : (c + 1) * low] = tiles[c, r]
    work[:, size:] = (
        lax.broadcasted_iota(jnp.int32, (size, size), 0)
        == lax.broadcasted_iota(jnp.int32, (size, size), 1)
    ).astype(F32)

    blocks = size // NB
    for b in range(blocks):
        factor_block(work, upper, size, NB, b)
        if b == 0:
            if relay:
                for copy in (early[0], late[0], early[1], late[1]):
                    copy.wait_recv()
                for copy in forwards:
                    copy.start()
    lower[...] = upper[...].T
    inverse[...] = work[:, size:]

    @pl.when(lax.rem(row, 2) != lax.rem(my_root, 2))
    def _():
        for c in range(cols):
            strip_sends(c)[2][1].wait_recv()

    strip[...] = jnp.dot(
        work[:, size:],
        strip_all[...].reshape(size, size),
        precision=HI,
        preferred_element_type=F32,
    )
    for c in range(cols):
        give, copy = strip_give(c)
        pl.when(give)(copy.wait_send)
        for cond, copy in strip_sends(c):
            pl.when(cond)(copy.wait_send)
    own_panel.wait()
    for copy in early + late:
        copy.wait_send()
    for copy in late[2:] if relay else late:
        copy.wait_recv()
    for copy in forwards:
        copy.wait()


def split(x):
    high = x.astype(jnp.bfloat16)
    return high, (x - high.astype(F32)).astype(jnp.bfloat16)


def dot_split(a, b):
    (ah, al), (bh, bl) = a, b
    dot = functools.partial(jnp.dot, preferred_element_type=F32)
    return dot(ah, bh) + (dot(ah, bl) + dot(al, bh))


def update_kernel(
    rows, cols, group, gathered, inverse, strip, lower, slab, diag_out, panel_out, slab_out,
    inv_high, inv_low, strip_high, strip_low,
):
    row, col = lax.axis_index("prow"), lax.axis_index("pcol")
    step, size = pl.program_id(0), strip.shape[0]
    high, low = diag_out.shape
    count = slab.shape[0] // size

    @pl.when(step == 0)
    def _():
        inv_high[...], inv_low[...] = split(inverse[...])
        strip_high[...], strip_low[...] = split(strip[...])

    full = gathered[...].reshape(size, count * size)
    factor = dot_split((inv_high[...], inv_low[...]), split(full))
    for c in range(cols):

        @pl.when(col == c)
        def _():
            panel_out[...] = factor[c * low : (c + 1) * low, :]

            @pl.when(step == 0)
            def _():
                start = pl.multiple_of(row * high, high)
                diag_out[...] = lower[pl.ds(start, high), c * low : (c + 1) * low]

    product = dot_split(split(factor.T), (strip_high[...], strip_low[...]))
    for i in range(count):
        here = slice(i * size, (i + 1) * size)
        shift = ((step * count + i) * rows + row - col * group) * size
        shape = (size, slab.shape[1])
        keep = (
            lax.broadcasted_iota(jnp.int32, shape, 0) + shift
            >= lax.broadcasted_iota(jnp.int32, shape, 1)
        )
        slab_out[here, :] = jnp.where(keep, slab[here, :] - product[here, :], slab[here, :])


def local(rows, cols, diag_block, panel, slab):
    high, low = diag_block.shape
    size = high * rows
    local_rows, width = panel.shape
    blocks = local_rows // size
    group = blocks * rows // cols
    any_spec = pl.BlockSpec(memory_space=pl.ANY)
    vmem = pl.BlockSpec(memory_space=pltpu.VMEM)
    dma = pltpu.SemaphoreType.DMA
    square = jax.ShapeDtypeStruct((size, size), F32)
    gathered, lower, inverse, strip = pl.pallas_call(
        functools.partial(gather_kernel, rows, cols, group),
        out_shape=[jax.ShapeDtypeStruct((cols, width, local_rows), F32), square, square, square],
        in_specs=[vmem, any_spec],
        out_specs=[any_spec, vmem, vmem, vmem],
        scratch_shapes=[
            pltpu.VMEM((cols, rows, high, low), F32),
            pltpu.VMEM((size, 2 * size), F32),
            pltpu.VMEM((size, size), F32),
            pltpu.VMEM((cols, width, size), F32),
            dma((rows,)), dma((rows,)), dma((cols,)), dma((cols,)), dma((3,)),
            dma((cols, 4)), dma((cols, 4)), dma((cols, 3)), dma((cols,)),
            dma((cols,)), dma((cols,)), dma((cols,)),
        ],
        compiler_params=pltpu.CompilerParams(collective_id=0, has_side_effects=True),
        name="gather_factor",
    )(diag_block, panel.T)
    tile = TILE if blocks % TILE == 0 else 1
    whole = pl.BlockSpec((size, size), lambda i: (0, 0))
    diag_out, panel_out, slab_out = pl.pallas_call(
        functools.partial(update_kernel, rows, cols, group),
        grid=(blocks // tile,),
        out_shape=[
            jax.ShapeDtypeStruct(diag_block.shape, F32),
            jax.ShapeDtypeStruct((width, local_rows), F32),
            jax.ShapeDtypeStruct(slab.shape, F32),
        ],
        in_specs=[
            pl.BlockSpec((cols, width, tile * size), lambda i: (0, 0, i)),
            whole,
            whole,
            whole,
            pl.BlockSpec((tile * size, slab.shape[1]), lambda i: (i, 0)),
        ],
        out_specs=[
            pl.BlockSpec((high, low), lambda i: (0, 0)),
            pl.BlockSpec((width, tile * size), lambda i: (0, i)),
            pl.BlockSpec((tile * size, slab.shape[1]), lambda i: (i, 0)),
        ],
        scratch_shapes=[pltpu.VMEM((size, size), jnp.bfloat16)] * 4,
        name="update",
    )(gathered, inverse, strip, lower, slab)
    return diag_out, panel_out.T, slab_out


def solution(mesh):
    spec = P("prow", "pcol")
    return jax.shard_map(
        functools.partial(local, mesh.shape["prow"], mesh.shape["pcol"]),
        mesh=mesh,
        in_specs=(spec, spec, spec),
        out_specs=(spec, spec, spec),
        check_vma=False,
    )
```
